32 devices in a mesh: leaf: 4 (over y, x), row: 2 (over core), col: 4 (over z).
Axes of the slice: x: 2, y: 2, z: 4, core: 2. Of those that a mesh axis runs over, the one named last changes fastest.
Arguments:
- anc_inverse: float32 [24, 24, 512, 512], P('leaf', None, 'row', 'col'), may hold values from -6 to 6, as said below
- struct_one: int32 [12, 5], P('leaf'), may hold values from 0 to 23, as said below
- lower_one: float32 [12, 5, 512, 512], P('leaf', None, 'row', 'col'), may hold values from -0.125 to 0.125
- pivot_inv_one: float32 [12, 512, 512], P('leaf', 'row', 'col'), may hold values from -6 to 6, as said below
- lower_two: float32 [24, 6, 512, 512], P('leaf', None, 'row', 'col'), may hold values from -0.109375 to 0.109375
- pivot_inv_two: float32 [24, 512, 512], P('leaf', 'row', 'col'), may hold values from -6 to 6, as said below
Outputs:
- offdiag_one: float32 [12, 5, 512, 512], P('leaf', None, 'row', 'col')
- diag_one: float32 [12, 512, 512], P('leaf', 'row', 'col')
- offdiag_two: float32 [24, 6, 512, 512], P('leaf', None, 'row', 'col')
- diag_two: float32 [24, 512, 512], P('leaf', 'row', 'col')
The draws below stay inside these ranges and needn't reach their ends.
Inputs may be any that keep to these rules, and one draw needn't show every extreme that they name: `struct_one`: each row lists 5 different separator block numbers in increasing order. symmetric: anc_inverse[b, a] is the transpose of anc_inverse[a, b]. `pivot_inv_one`: every block equals its transpose. `pivot_inv_two`: every block equals its transpose.
All inputs are finite; a program needn't handle non-finite values.
Results may differ from the reference program's by a relative error of at most 0.0001.
Values sent between devices are 32-bit elements; how exact they have to be, the bound alone decides.
No kernel may reach another device: no remote copies, remote signals or barrier semaphores. Data moves between devices by JAX's collectives and lax.ppermute only.
A program may use at most 192 MiB of HBM per device.

```python
import jax
import jax.numpy as jnp
from jax import lax

W = 512
NA = 24
SK1 = 5
K2 = 2
NODES1 = 12
NODES2 = 24


def draw_struct_one(key, part):
    row_keys = jax.random.split(jax.random.fold_in(key, 17), NODES1)

    def one_row(row_key):
        return jax.random.permutation(row_key, NA)
    shuffled = jax.vmap(one_row)(row_keys)
    return jnp.sort(shuffled[:, :SK1], axis=1).astype(jnp.int32)


def raw_values(key, shape):
    return jax.random.normal(key, shape, jnp.float32)


def draw_anc_inverse(key, part):
    values = raw_values(jax.random.fold_in(key, 31), (NA, NA, W, W))
    both = (values + jnp.transpose(values, (1, 0, 3, 2))) * 0.70710678
    return jnp.clip(both, -6.0, 6.0)


def symmetric_pivots(key, count):
    values = raw_values(key, (count, W, W))
    both = (values + jnp.transpose(values, (0, 2, 1))) * 0.70710678
    return jnp.clip(both, -6.0, 6.0)


def draw_pivot_inv_one(key, part):
    return symmetric_pivots(jax.random.fold_in(key, 41), NODES1)


def draw_pivot_inv_two(key, part):
    return symmetric_pivots(jax.random.fold_in(key, 43), NODES2)


def block_levels(own_key, shape, pieces, low, top_value):
    level, own = 1.0, jax.random.fold_in(own_key, 6)
    for axis_at, shards_of in pieces:
        steps = jnp.exp(jax.random.uniform(jax.random.fold_in(own, axis_at), (shards_of,), jnp.float32, low / len(pieces), top_value / len(pieces)))
        level = level * jnp.repeat(steps, shape[axis_at] // shards_of).reshape([-1 if axis == axis_at else 1 for axis in range(len(shape))])
    return level


def gaussian(key, shape, scale, bound, cuts=(), kind=jnp.bfloat16):
    values = jax.random.normal(key, shape, jnp.float32) * scale
    if len(cuts) > 0:
        values = block_levels(key, shape, cuts, -0.22, 0.18) * values
    return jnp.clip(values, min=-bound, max=bound).astype(kind)


def setup_inputs(seed: int = 0) -> dict:
    seeds = jax.random.split(jax.random.key(seed), 7)
    return {
        "anc_inverse": draw_anc_inverse(jax.random.fold_in(seeds[6], 71), 0),
        "struct_one": draw_struct_one(jax.random.fold_in(seeds[6], 71), 0),
        "lower_one": gaussian(seeds[2], (NODES1, SK1, W, W), (SK1 * W) ** -0.5, 0.125, ((0, 4), (2, 2), (3, 4)), jnp.float32),
        "pivot_inv_one": draw_pivot_inv_one(jax.random.fold_in(seeds[6], 71), 0),
        "lower_two": gaussian(seeds[4], (NODES2, SK1 + 1, W, W), ((SK1 + 1) * W) ** -0.5, 0.109375, ((0, 4), (2, 2), (3, 4)), jnp.float32),
        "pivot_inv_two": draw_pivot_inv_two(jax.random.fold_in(seeds[6], 71), 0),
    }


highest = lax.Precision.HIGHEST


def reference(anc_inverse, struct_one, lower_one, pivot_inv_one, lower_two, pivot_inv_two):
    outs_one = []
    diags_one = []
    outs_two = []
    diags_two = []
    for supernode in range(NODES1):
        listed = struct_one[supernode].astype(jnp.int32)
        picked = anc_inverse[listed[:, None], listed[None, :]]
        offdiag = -jnp.einsum("stik,tkj->sij", picked, lower_one[supernode], precision=highest)
        diagonal = pivot_inv_one[supernode] - jnp.einsum("ski,skj->ij", lower_one[supernode], offdiag, precision=highest)
        outs_one.append(offdiag)
        diags_one.append(diagonal)
        upper_rows = jnp.concatenate([picked, offdiag[:, None]], axis=1)
        last_row = jnp.concatenate([jnp.swapaxes(offdiag, 1, 2), diagonal[None]], axis=0)[None]
        known_inverse = jnp.concatenate([upper_rows, last_row], axis=0)
        for child in range(K2):
            factor = lower_two[supernode * K2 + child]
            offdiag_child = -jnp.einsum("pqik,qkj->pij", known_inverse, factor, precision=highest)
            diag_child = pivot_inv_two[supernode * K2 + child] - jnp.einsum("pki,pkj->ij", factor, offdiag_child, precision=highest)
            outs_two.append(offdiag_child)
            diags_two.append(diag_child)
    return jnp.stack(outs_one), jnp.stack(diags_one), jnp.stack(outs_two), jnp.stack(diags_two)
```

```python
import jax
import jax.numpy as jnp
from jax import lax
from jax.experimental import pallas as pl
from jax.experimental.pallas import tpu as pltpu
from jax.sharding import PartitionSpec as P


def select(anc, rows, cols):
    owned, blocks, tr, tc = anc.shape
    dests, pairs = rows.shape
    group = max(n for n in range(1, 6) if pairs % n == 0)
    have = (rows >= 0) & (rows < owned)
    index = jnp.where(have, rows * blocks + cols, 0).reshape(-1)
    flat = anc.reshape(owned * blocks, tr, tc)

    def kernel(index_ref, have_ref, *refs):
        out = refs[group]
        for j in range(group):
            keep = have_ref[pl.program_id(0) * group + j]

            @pl.when(keep == 1)
            def _():
                out[j] = refs[j][0]

            @pl.when(keep == 0)
            def _():
                out[j] = jnp.zeros((tr, tc), jnp.float32)

    def block(j):
        return pl.BlockSpec((1, tr, tc), lambda g, i, h: (i[g * group + j], 0, 0))

    return pl.pallas_call(
        kernel,
        grid_spec=pltpu.PrefetchScalarGridSpec(
            num_scalar_prefetch=2,
            grid=(dests * pairs // group,),
            in_specs=[block(j) for j in range(group)],
            out_specs=pl.BlockSpec((group, tr, tc), lambda g, i, h: (g, 0, 0)),
        ),
        out_shape=jax.ShapeDtypeStruct((dests * pairs, tr, tc), anc.dtype),
        name="select_blocks",
    )(index, have.astype(jnp.int32).reshape(-1), *[flat] * group).reshape(dests, pairs, tr, tc)


def split(value):
    top = value.astype(jnp.bfloat16)
    return top, (value - top.astype(jnp.float32)).astype(jnp.bfloat16)


def split_dot(left, right, dims):
    def product(x, y):
        return lax.dot_general(x, y, (dims, ((), ())), preferred_element_type=jnp.float32)

    (left_top, left_low), (right_top, right_low) = left, right
    return product(left_top, right_top) + (
        product(left_top, right_low) + product(left_low, right_top)
    )


def by_position(where, pieces, out, sems, size):
    tc = pieces[0].shape[2]
    for at in range(size):
        for here in range(size):

            @pl.when(where == here)
            def _():
                pltpu.make_async_copy(
                    pieces[size - 1 + at - here],
                    out.at[:, :, pl.ds(at * tc, tc)],
                    sems.at[at],
                ).start()


def wait_positions(pieces, out, sems, size):
    tc = pieces[0].shape[2]
    for at in range(size):
        pltpu.make_async_copy(
            pieces[size - 1], out.at[:, :, pl.ds(at * tc, tc)], sems.at[at]
        ).wait()


anywhere = pl.BlockSpec(memory_space=pl.ANY)
scalars = pl.BlockSpec(memory_space=pltpu.SMEM)
local = pl.BlockSpec(memory_space=pltpu.VMEM)
row_row = ((0,), (0,))
plain = ((1,), (0,))


def change_base(parts, two, t_rows, place, size):
    count, tr, tc = parts[0].shape
    length = count - 1
    children = two.shape[0]
    many = len(parts)

    def kernel(where, *refs):
        pieces = refs[:many]
        two_ref, t_ref, right, pivot, full, held, sems = refs[many:]
        by_position(where[0], pieces, held, sems, size)
        terms = [split(t_ref[k]) for k in range(children)]
        wait_positions(pieces, held, sems, size)

        for k in range(children):
            pivot[k] = split_dot(split(held[length]), terms[k], plain)

        for s in range(length):
            whole = held[s]
            full[s] = whole
            both = split(whole)
            for k in range(children):
                changed = two_ref[k, s] - split_dot(both, terms[k], plain)
                right[s, :, pl.ds((k + 1) * tc, tc)] = changed
        for here in range(size):

            @pl.when(where[0] == here)
            def _():
                right[:, :, pl.ds(0, tc)] = held[pl.ds(0, length), :, pl.ds(here * tc, tc)]

    shape = lambda *dims: jax.ShapeDtypeStruct(dims, jnp.float32)
    return pl.pallas_call(
        kernel,
        in_specs=[scalars] + [anywhere] * many + [local, local],
        out_specs=(local, local, local),
        out_shape=(
            shape(length, tr, (children + 1) * tc),
            shape(children, tr, tc),
            shape(length, tr, size * tc),
        ),
        scratch_shapes=[
            pltpu.VMEM((count, tr, size * tc), jnp.float32),
            pltpu.SemaphoreType.DMA((size,)),
        ],
        name="change_base",
    )(place.reshape(1), *parts, two, t_rows)


def share(whole, keep, sends, row_at, tr, axis):
    for step, out in enumerate([keep, *sends]):
        owner = lax.rem(row_at + step, len(sends) + 1)
        rows = pl.ds(pl.multiple_of(owner * tr, tr), tr)
        out[...] = whole[rows] if axis == 0 else whole[:, rows]


def multiply(parts, rights, place, row_place, table, size):
    count, tr, tc = parts[0].shape
    length, _, wide = rights[0].shape
    width = size * tc
    many, shares = len(parts), len(rights)

    def kernel(where, row_at, pair, *refs):
        pieces, given = refs[:many], refs[many : many + shares]
        direct, top, low, *outs = refs[many + shares : -3]
        held, turned, sems = refs[-3:]
        by_position(where[0], pieces, held, sems, size)
        for step, right in enumerate(given):
            owner = lax.rem(row_at[0] + shares - step, shares)
            rows = pl.ds(pl.multiple_of(owner * tr, tr), tr)
            for p in range(length):
                top[p, rows], low[p, rows] = split(right[p])
        direct[...] = jnp.zeros_like(direct)
        turned[...] = jnp.zeros_like(turned)
        start = pl.multiple_of(row_at[0] * tr, tr)
        wait_positions(pieces, held, sems, size)

        def step(t, carry):
            p, q = pair[0, t], pair[1, t]
            block = split(held[t])
            direct[p] += split_dot(block, (top[q], low[q]), plain)
            mine = (top[p, pl.ds(start, tr)], low[p, pl.ds(start, tr)])
            turned[q - 1] += split_dot(block, mine, row_row)
            return carry

        lax.fori_loop(0, count, step, 0)
        share(turned, outs[0], outs[1:], row_at[0], tr, 1)

    return pl.pallas_call(
        kernel,
        in_specs=[scalars] * 3 + [anywhere] * many + [local] * shares,
        out_specs=(local,) * (3 + shares),
        out_shape=(
            jax.ShapeDtypeStruct((length, tr, wide), jnp.float32),
            jax.ShapeDtypeStruct((length, width, wide), jnp.bfloat16),
            jax.ShapeDtypeStruct((length, width, wide), jnp.bfloat16),
            *[jax.ShapeDtypeStruct((length - 1, tr, wide), jnp.float32)] * shares,
        ),
        scratch_shapes=[
            pltpu.VMEM((count, tr, width), jnp.float32),
            pltpu.VMEM((length - 1, width, wide), jnp.float32),
            pltpu.SemaphoreType.DMA((size,)),
        ],
        name="multiply",
    )(place.reshape(1), row_place.reshape(1), table, *parts, *rights)


def finish(parts, top, low, direct, turned, one_full, place, row_place, size, before, m, nodes):
    length, tr, wide = direct.shape
    width = top.shape[1]
    tc = parts[0].shape[2]
    many, shares = len(parts), len(turned)
    chained = [] if before is None else [before]
    fixed = many + 4 + shares

    def kernel(where, row_at, *refs):
        pieces = refs[:many]
        top_ref, low_ref, direct_ref, one_ref = refs[many : many + 4]
        sums = refs[many + 4 : fixed]
        product, off, *outs = refs[fixed + len(chained) : -5]
        held, staged, below, sems, sem = refs[-5:]
        by_position(where[0], pieces, held, sems, size)
        below[...] = jnp.zeros_like(below)
        product[0] = direct_ref[0]
        for p in range(1, length):
            value = direct_ref[p]
            for turned_ref in sums:
                value = value + turned_ref[p - 1]
            product[p] = value
        wait_positions(pieces, held, sems, size)

        def step(p, carry):
            value = product[p] + split_dot(split(held[p]), (top_ref[p], low_ref[p]), plain)
            product[p] = value
            staged[p] = -value[:, :tc]
            below[...] += split_dot(split(one_ref[p]), split(value), row_row)
            return carry

        lax.fori_loop(0, length, step, 0)
        out = pltpu.make_async_copy(staged, off.at[m], sem)
        out.start()
        share(below, outs[0], outs[1:], row_at[0], tr, 0)
        out.wait()

    shape = lambda *dims: jax.ShapeDtypeStruct(dims, jnp.float32)
    return pl.pallas_call(
        kernel,
        in_specs=[scalars] * 2
        + [anywhere] * many
        + [local] * (4 + shares)
        + [anywhere] * len(chained),
        out_specs=(local, anywhere) + (local,) * shares,
        out_shape=(
            shape(length, tr, wide),
            shape(nodes, length, tr, tc),
            *[shape(tr, wide)] * shares,
        ),
        scratch_shapes=[
            pltpu.VMEM((length, tr, width), jnp.float32),
            pltpu.VMEM((length, tr, tc), jnp.float32),
            pltpu.VMEM((width, wide), jnp.float32),
            pltpu.SemaphoreType.DMA((size,)),
            pltpu.SemaphoreType.DMA,
        ],
        input_output_aliases={2 + fixed: 1} if chained else {},
        name="finish",
    )(
        place.reshape(1), row_place.reshape(1), *parts, top, low, direct, one_full, *turned,
        *chained,
    )


def symmetric_upper(product, pieces, holders, place):
    length, tr, _ = product.shape
    keys = sorted(pieces)
    tc = pieces[keys[0]].shape[2]

    def kernel(where, product_ref, *refs):
        given, out = dict(zip(keys, refs)), refs[-1]
        for k in sorted({j for j, _ in keys}):
            column = product_ref[:, :, pl.ds((k + 1) * tc, tc)]
            column = split(column.reshape(length * tr, tc))
            for index, key in enumerate(keys):
                if key[0] != k:
                    continue
                used = where[0] == holders[key][0]
                for here in holders[key][1:]:
                    used = used | (where[0] == here)

                @pl.when(used)
                def _():
                    piece = split(given[key][...].reshape(length * tr, tc))
                    out[index] = split_dot(piece, column, row_row)

    block = pl.BlockSpec((length, tr, tc), lambda i: (0, 0, 0))
    return pl.pallas_call(
        kernel,
        grid=(1,),
        in_specs=[scalars, pl.BlockSpec(product.shape, lambda i: (0, 0, 0))]
        + [block] * len(keys),
        out_specs=pl.BlockSpec((len(keys), tc, tc), lambda i: (0, 0, 0)),
        out_shape=jax.ShapeDtypeStruct((len(keys), tc, tc), jnp.float32),
        name="symmetric_upper",
    )(place.reshape(1), product, *[pieces[key] for key in keys])


def symmetric_last(
    product, below, pivot, own_pivot, upper, pieces, holders, place, size, before, m, nodes
):
    length, tr, wide = product.shape
    children = pivot.shape[0]
    tc = pivot.shape[2]
    keys = sorted(pieces)
    chained = [] if before is None else [before]
    shares = len(below)

    def kernel(where, product_ref, pivot_ref, own_ref, upper_ref, *refs):
        parts, given = refs[:shares], dict(zip(keys, refs[shares:]))
        diag, base, off, out, staged, total, sem = refs[shares + len(keys) + len(chained) :]
        value = parts[0][...]
        for part in parts[1:]:
            value = value + part[...]
        total[...] = value
        for k in range(children):
            span = pl.ds((k + 1) * tc, tc)
            staged[k, pl.ds(0, length)] = -product_ref[:, :, span]
            staged[k, length] = total[:, span] - pivot_ref[k]
        copy = pltpu.make_async_copy(staged, off.at[m], sem)
        copy.start()
        diag[...] = own_ref[...] + total[:, pl.ds(0, tc)]
        base[...] = jnp.zeros_like(base)
        out[...] = jnp.zeros_like(out)
        for k in range(children):
            column = split(pivot_ref[k] - total[:, pl.ds((k + 1) * tc, tc)])
            for index, (j, away) in enumerate(keys):
                if j != k:
                    continue
                for here in holders[k, away]:

                    @pl.when(where[0] == here)
                    def _():
                        piece = split(given[k, away][0])
                        tile = upper_ref[index] + split_dot(piece, column, row_row)
                        base[here + away, k] = tile
                        if away != 0:
                            out[away % size - 1, k] = tile.T

        copy.wait()

    shape = lambda *dims: jax.ShapeDtypeStruct(dims, jnp.float32)
    whole = lambda value: pl.BlockSpec(value.shape, lambda i: (0,) * len(value.shape))
    block = pl.BlockSpec((1, tr, tc), lambda i: (length, 0, 0))
    shapes = [
        shape(tr, tc),
        shape(size, children, tc, tc),
        shape(nodes, children, length + 1, tr, tc),
        shape(size - 1, children, tc, tc),
    ]
    inputs = [product, pivot, own_pivot, upper, *below]
    diag, base, off, out = pl.pallas_call(
        kernel,
        grid=(1,),
        in_specs=[scalars, *map(whole, inputs), *[block] * len(keys), *[anywhere] * len(chained)],
        out_specs=tuple(anywhere if i == 2 else whole(o) for i, o in enumerate(shapes)),
        out_shape=tuple(shapes),
        scratch_shapes=[
            pltpu.VMEM((children, length + 1, tr, tc), jnp.float32),
            pltpu.VMEM((tr, wide), jnp.float32),
            pltpu.SemaphoreType.DMA,
        ],
        input_output_aliases={1 + len(inputs) + len(keys): 2} if chained else {},
        name="symmetric_last",
    )(place.reshape(1), *inputs, *[pieces[key] for key in keys], *chained)
    return off, diag, base, out


def put_back(base, got, place, row_place, tr, shares):
    size, children, tc, _ = base.shape

    def kernel(where, row_at, base_ref, *refs):
        given, outs, whole = refs[: size - 1], refs[size - 1 : -1], refs[-1]
        for k in range(children):
            for at in range(size):
                whole[k, pl.ds(at * tc, tc)] = base_ref[at, k]
            for step in range(1, size):
                source = lax.rem(where[0] + size - step, size)
                rows = pl.ds(pl.multiple_of(source * tc, tc), tc)
                whole[k, rows] += given[step - 1][k]
        share(whole, outs[0], outs[1:], row_at[0], tr, 1)

    return pl.pallas_call(
        kernel,
        in_specs=[scalars] * 2 + [local] * size,
        out_specs=(local,) * shares,
        out_shape=(jax.ShapeDtypeStruct((children, tr, tc), jnp.float32),) * shares,
        scratch_shapes=[pltpu.VMEM((children, size * tc, tc), jnp.float32)],
        name="put_back",
    )(place.reshape(1), row_place.reshape(1), base, *got)


def along_row(value, step):
    count = lax.axis_size("row")
    return lax.ppermute(value, "row", [(i, (i + step) % count) for i in range(count)])


def spread(keep, sends):
    return [keep] + [along_row(value, step + 1) for step, value in enumerate(sends)]


def hop(value, pairs):
    return lax.ppermute(value, "col", pairs)


def line_gather(value, size):
    rights, lefts = [value], [value]
    for step in range(1, size):
        rights.append(hop(rights[-1], [(i, i + 1) for i in range(step - 1, size - 1)]))
        lefts.append(hop(lefts[-1], [(i + 1, i) for i in range(size - step)]))
    return rights[:0:-1] + lefts


def computes(low, high_at, child, size):
    off_low, off_high = abs(2 * low - size + 1), abs(2 * high_at - size + 1)
    if off_low == off_high:
        return high_at if child % 2 == 0 else low
    return low if off_low < off_high else high_at


def pair_gather(value, child, size):
    pieces, holders = {0: value}, {0: list(range(size))}
    for sign in (1, -1):
        moving = value
        for step in range(1, size):
            pairs, uses = [], []
            for source in range(size):
                ends = [
                    end
                    for end in range(size)
                    if (end - source) * sign >= step
                    and computes(min(source, end), max(source, end), child, size) == end
                ]
                if ends:
                    pairs.append((source + sign * (step - 1), source + sign * step))
                    if source + sign * step in ends:
                        uses.append(source + sign * step)
            if not pairs:
                break
            moving = hop(moving, pairs)
            if uses:
                pieces[-sign * step], holders[-sign * step] = moving, uses
    return pieces, holders


def on_device(anc_inverse, struct_one, lower_one, pivot_inv_one, lower_two, pivot_inv_two):
    nodes, length = struct_one.shape
    owned = anc_inverse.shape[0]
    tr, tc = lower_one.shape[2:]
    children = lower_two.shape[0] // nodes
    size, place = lax.axis_size("col"), lax.axis_index("col")
    row_place = lax.axis_index("row")
    two = lower_two.reshape(nodes, children, length + 1, tr, tc)
    apart = [(p, q) for p in range(length) for q in range(p + 1, length)]
    pairs = apart + [(p, p) for p in range(length)]
    first = jnp.array([p for p, _ in pairs], jnp.int32)
    second = jnp.array([q for _, q in pairs], jnp.int32)
    table = jnp.stack([first, second])

    pieces_one = [
        line_gather(jnp.concatenate([lower_one[m], pivot_inv_one[m][None]]), size)
        for m in range(nodes)
    ]
    lists = lax.all_gather(struct_one, "leaf", axis=0, tiled=False)
    near = lists - lax.axis_index("leaf") * owned
    t_rows = lax.all_gather(two[:, :, length], "row", axis=2, tiled=True)
    picked = []
    for m in range(nodes):
        parts = []
        for span in (slice(0, len(apart)), slice(len(apart), len(pairs))):
            mine = select(
                anc_inverse, near[:, m][:, first[span]], lists[:, m][:, second[span]]
            )
            parts.append(lax.psum_scatter(mine, "leaf", scatter_dimension=0, tiled=False))
        picked.append(parts)
    given, holders = [], {}
    for m in range(nodes):
        pieces = {}
        for k in range(children):
            found, uses = pair_gather(two[m, k], k, size)
            for away, piece in found.items():
                pieces[k, away], holders[k, away] = piece, uses[away]
        given.append(pieces)
    bases = []
    for m in range(nodes):
        bases.append(change_base(pieces_one[m], two[m], t_rows[m], place, size))
    off_one, off_two = None, None
    diags_one, diags_two = [], []
    shares = lax.axis_size("row")
    for m in range(nodes):
        right, pivot, one_full = bases[m]
        rights = spread(right, [right] * (shares - 1))
        apart_parts = line_gather(picked[m][0], size)
        same_parts = line_gather(picked[m][1], size)
        direct, top, low, *turned = multiply(
            apart_parts, rights, place, row_place, table, size
        )
        turned = spread(turned[0], turned[1:])
        product, off_one, *below = finish(
            same_parts, top, low, direct, turned, one_full, place, row_place, size,
            off_one, m, nodes,
        )
        below = spread(below[0], below[1:])
        upper = symmetric_upper(product, given[m], holders, place)
        off_two, diag_one, base, sends = symmetric_last(
            product, below, pivot, pivot_inv_one[m], upper, given[m], holders,
            place, size, off_two, m, nodes,
        )
        got = []
        for step in range(1, size):
            moves = [
                (here, (here + away) % size)
                for (_, away), uses in holders.items()
                for here in uses
                if away != 0 and away % size == step
            ]
            got.append(hop(sends[step - 1], sorted(set(moves))))
        keep, *sends = put_back(base, got, place, row_place, tr, shares)
        summed = spread(keep, sends)
        diags_one.append(diag_one)
        diags_two.append(pivot_inv_two.reshape(nodes, children, tr, tc)[m] + sum(summed[1:], summed[0]))
    return (
        off_one,
        jnp.stack(diags_one),
        off_two.reshape(lower_two.shape),
        jnp.stack(diags_two).reshape(pivot_inv_two.shape),
    )


def solution(mesh):
    placed = (
        P("leaf", None, "row", "col"),
        P("leaf", None),
        P("leaf", None, "row", "col"),
        P("leaf", "row", "col"),
        P("leaf", None, "row", "col"),
        P("leaf", "row", "col"),
    )
    return jax.shard_map(
        on_device,
        mesh=mesh,
        in_specs=placed,
        out_specs=(
            P("leaf", None, "row", "col"),
            P("leaf", "row", "col"),
            P("leaf", None, "row", "col"),
            P("leaf", "row", "col"),
        ),
        check_vma=False,
    )
```
